32 devices in a mesh: base: 16 (over z, x, core), band: 2 (over y).
Axes of the slice: x: 2, y: 2, z: 4, core: 2. Of those that a mesh axis runs over, the one named last changes fastest.
Arguments:
- coherency: float32 [16, 16, 8, 4096], P('band', None, None, 'base'), may hold values from -1.5 to 1.5
- observed: float32 [16, 8, 4096], P('band', None, 'base'), may hold values from -6 to 6
- jones_deviation: float32 [16, 16, 8, 512], P('band', None, None, 'base'), may hold values from -1.8 to 1.8
- antenna_first: int32 [4096], P('base'), may hold values from 0 to 511, as said below
- antenna_second: int32 [4096], P('base'), may hold values from 0 to 511, as said below
Outputs:
- jones: float32 [16, 16, 8, 512], P('band', None, None, 'base')
- residual: float32 [16, 8, 4096], P('band', None, 'base')
The draws below stay inside these ranges and needn't reach their ends.
Inputs may be any that keep to these rules, and one draw needn't show every extreme that they name: `antenna_first`: every station is the first station of exactly 8 baselines. On every baseline antenna_second differs from antenna_first.
All inputs are finite; a program needn't handle non-finite values.
Results may differ from the reference program's by a relative error of at most 0.0003.
Values sent between devices are 32-bit elements; how exact they have to be, the bound alone decides.
A program may use at most 128 MiB of HBM per device.

```python
import jax
import jax.numpy as jnp
from jax import lax

STATION_TOTAL = 512
DIRECTION_COUNT = 16
SUBBAND_COUNT = 16
ITERS = 3
BASELINE_TOTAL = 4096


def station_pairs(key):
    base_key = jax.random.fold_in(key, 11)
    leading_key = jax.random.fold_in(base_key, 1)
    iteration_key = jax.random.fold_in(base_key, 2)
    first_station = jax.random.permutation(leading_key, jnp.arange(BASELINE_TOTAL, dtype=jnp.int32) % STATION_TOTAL)
    deviation_values = jax.random.randint(iteration_key, (BASELINE_TOTAL,), 1, STATION_TOTAL, dtype=jnp.int32)
    second = (first_station + deviation_values) % STATION_TOTAL
    return (first_station.astype(jnp.int32), second.astype(jnp.int32))


def draw_antenna_first(key, part):
    return station_pairs(key)[0]


def draw_antenna_second(key, part):
    return station_pairs(key)[1]


def shard_levels(rng, dims, shards, least, largest):
    loudness = 1.0
    for axis_at, parts in shards:
        heights = jax.random.uniform(jax.random.fold_in(jax.random.fold_in(rng, 6), axis_at), (parts,), jnp.float32, least / len(shards), largest / len(shards))
        loudness = loudness * jnp.repeat(jnp.exp(heights), dims[axis_at] // parts).reshape((-1,) + (1,) * (len(dims) - 1 - axis_at))
    return loudness


def centred(own_key, shape, deviation, limit, cuts=(), kind=jnp.bfloat16):
    result = deviation * jax.random.normal(own_key, shape, jnp.float32)
    if cuts:
        result = result * shard_levels(own_key, shape, cuts, -0.22, 0.18)
    return jnp.clip(result, -limit, limit).astype(kind)


def setup_inputs(seed: int = 0) -> dict:
    key_list = jax.random.split(jax.random.key(seed), 6)
    return {
        "coherency": centred(key_list[0], (SUBBAND_COUNT, DIRECTION_COUNT, 8, BASELINE_TOTAL), 0.25, 1.5, ((0, 2), (3, 16)), jnp.float32),
        "observed": centred(key_list[1], (SUBBAND_COUNT, 8, BASELINE_TOTAL), 1.0, 6.0, ((0, 2), (2, 16)), jnp.float32),
        "jones_deviation": centred(key_list[2], (SUBBAND_COUNT, DIRECTION_COUNT, 8, STATION_TOTAL), 0.3, 1.8, ((0, 2), (3, 16)), jnp.float32),
        "antenna_first": draw_antenna_first(jax.random.fold_in(key_list[5], 71), 0),
        "antenna_second": draw_antenna_second(jax.random.fold_in(key_list[5], 71), 0),
    }


step_gain = 1.2
penalty_gain = 0.25

def expand_matrix(packed):
    return [[(packed[..., 0, :], packed[..., 1, :]), (packed[..., 2, :], packed[..., 3, :])], [(packed[..., 4, :], packed[..., 5, :]), (packed[..., 6, :], packed[..., 7, :])]]

def pack_matrix(matrix):
    return jnp.stack([matrix[0][0][0], matrix[0][0][1], matrix[0][1][0], matrix[0][1][1], matrix[1][0][0], matrix[1][0][1], matrix[1][1][0], matrix[1][1][1]], axis=-2)

def complex_mul(first_term, second_term):
    return (first_term[0] * second_term[0] - first_term[1] * second_term[1], first_term[0] * second_term[1] + first_term[1] * second_term[0])

def complex_add(first_term, second_term):
    return (first_term[0] + second_term[0], first_term[1] + second_term[1])

def element_of(matrix, i, j, adjoint):
    if adjoint:
        return (matrix[j][i][0], -matrix[j][i][1])
    return matrix[i][j]

def matrix_product(first_factor, second_factor, adjoint_first=False, adjoint_second=False):
    result_rows = []
    for i in range(2):
        row_items = []
        for j in range(2):
            row_items.append(complex_add(complex_mul(element_of(first_factor, i, 0, adjoint_first), element_of(second_factor, 0, j, adjoint_second)), complex_mul(element_of(first_factor, i, 1, adjoint_first), element_of(second_factor, 1, j, adjoint_second))))
        result_rows.append(row_items)
    return result_rows

def fit_basis(band_count):
    positions = (2.0 * jnp.arange(band_count, dtype=jnp.float32) + 1.0) / band_count - 1.0
    columns = []
    for power in range(4):
        vector = positions ** power
        for earlier in columns:
            vector = vector - jnp.sum(earlier * vector) * earlier
        vector = vector / jnp.sqrt(jnp.sum(vector * vector))
        columns.append(vector)
    return jnp.stack(columns, axis=1)

def subband_update(jones_full, coherency_model, visibility_data, antenna_first, antenna_second):
    leading_jones = expand_matrix(jnp.take(jones_full, antenna_first, axis=2))
    trailing_jones = expand_matrix(jnp.take(jones_full, antenna_second, axis=2))
    sky = expand_matrix(coherency_model)
    model = pack_matrix(matrix_product(leading_jones, matrix_product(sky, trailing_jones, adjoint_second=True)))
    residual = visibility_data - lax.optimization_barrier(jnp.sum(model, axis=0))
    resid_parts = expand_matrix(residual[None])
    gradient_leading = pack_matrix(matrix_product(resid_parts, matrix_product(trailing_jones, sky, adjoint_second=True)))
    gradient_trailing = pack_matrix(matrix_product(resid_parts, matrix_product(leading_jones, sky), adjoint_first=True))
    gradient_list = jnp.zeros_like(jones_full).at[:, :, antenna_first].add(gradient_leading).at[:, :, antenna_second].add(gradient_trailing)
    return (gradient_list, residual)

def reference(coherency, observed, jones_deviation, antenna_first, antenna_second):
    highest = lax.Precision.HIGHEST
    baseline_count = coherency.shape[-1]
    station_number = jones_deviation.shape[-1]
    step_size = step_gain * station_number / baseline_count
    penalty = penalty_gain * baseline_count / station_number
    poly_basis = fit_basis(coherency.shape[0])
    identity = jnp.array([1.0, 0.0, 0.0, 0.0, 0.0, 0.0, 1.0, 0.0], dtype=jnp.float32)[:, None]
    jones_current = identity + jones_deviation
    consensus = jones_current
    dual_var = jnp.zeros_like(jones_current)
    residual = None
    for iteration in range(ITERS):
        station_gradients, residual = lax.map(lambda entry_list: subband_update(entry_list[0], entry_list[1], entry_list[2], antenna_first, antenna_second), (jones_current, coherency, observed))
        jones_current = jones_current + step_size * (station_gradients - dual_var - penalty * (jones_current - consensus))
        if iteration + 1 < ITERS:
            target = jones_current + dual_var / penalty
            coefficients = jnp.einsum('fm,fkcs->mkcs', poly_basis, target, precision=highest)
            consensus = jnp.einsum('fm,mkcs->fkcs', poly_basis, coefficients, precision=highest)
            dual_var = dual_var + penalty * (jones_current - consensus)
    return (jones_current, residual)
```

```python
import functools

import jax
import jax.numpy as jnp
import numpy as np
from jax import lax
from jax.experimental import pallas as pl
from jax.experimental.pallas import tpu as pltpu
from jax.sharding import PartitionSpec as P

ITERS = 3
STEP_GAIN = 1.2
PENALTY_GAIN = 0.25
MESH = pl.DeviceIdType.MESH
HIGHEST = lax.Precision.HIGHEST


def fit_basis(band_count):
    positions = ((2.0 * np.arange(band_count) + 1.0) / band_count - 1.0).astype(np.float64)
    columns = []
    for power in range(4):
        vector = positions**power
        for earlier in columns:
            vector = vector - np.sum(earlier * vector) * earlier
        columns.append(vector / np.sqrt(np.sum(vector * vector)))
    return np.stack(columns, axis=1)


def components(x):
    n = x.shape[0] // 8
    c = [x[i * n : (i + 1) * n] for i in range(8)]
    return [[(c[0], c[1]), (c[2], c[3])], [(c[4], c[5]), (c[6], c[7])]]


def flat(m):
    return [m[i][j][p] for i in range(2) for j in range(2) for p in range(2)]


def cmul(a, b):
    return (a[0] * b[0] - a[1] * b[1], a[0] * b[1] + a[1] * b[0])


def element_of(m, i, j, adjoint):
    return (m[j][i][0], -m[j][i][1]) if adjoint else m[i][j]


def product(a, b, adjoint_a=False, adjoint_b=False):
    rows = []
    for i in range(2):
        row = []
        for j in range(2):
            u = cmul(element_of(a, i, 0, adjoint_a), element_of(b, 0, j, adjoint_b))
            v = cmul(element_of(a, i, 1, adjoint_a), element_of(b, 1, j, adjoint_b))
            row.append((u[0] + v[0], u[1] + v[1]))
        rows.append(row)
    return rows


def split_rows(x):
    high = x.astype(jnp.bfloat16)
    low = (x - high.astype(jnp.float32)).astype(jnp.bfloat16)
    return jnp.concatenate([high, low], axis=0)


def wait_bytes(ref, sem):
    pltpu.make_async_copy(ref, ref, sem).wait()


def kernel(
    cfg,
    coh, obs, dev, first, second,
    out_j, out_r,
    first_v, second_v, dev_v, obs_v, coh_v,
    onehot, cohc, left_t, right_t, model, model_r,
    jj, jones, dual, cons, acc,
    t_send, t_recv, z_send, z_recv, res, j_send,
    in_send, in_recv, coh_send, coh_recv,
    m_send, m_recv, ts_sem, tr_sem, zs_sem, zr_sem, o_send, o_recv,
):
    nb, nband, F, g, K, Kg, So, S, Bo, step, penalty, npc, lane_parts, groups = cfg
    rows = 8 * Kg
    N = F * nband
    L = S // lane_parts
    basis = fit_basis(N)
    me = lax.axis_index("base")
    mb = lax.axis_index("band")
    s = me // g
    r = me % g
    mine = mb * F + s
    cg = nb // groups

    barrier = pltpu.get_barrier_semaphore()

    def greet(o, _):
        pl.semaphore_signal(barrier, inc=1, device_id={"base": (me + o) % nb}, device_id_type=MESH)
        return 0

    lax.fori_loop(1, nb, greet, 0)
    for ob in range(1, nband):
        def greet_band(f, _):
            pl.semaphore_signal(
                barrier, inc=1,
                device_id={"band": (mb + ob) % nband, "base": f * g + r}, device_id_type=MESH,
            )
            return 0

        lax.fori_loop(0, F, greet_band, 0)
    pl.semaphore_wait(barrier, nb - 1 + F * (nband - 1))

    def small(kind, d):
        f = d // g
        k0 = (d % g) * Kg
        return [
            (first, first_v.at[me]),
            (second, second_v.at[me]),
            (dev.at[f, pl.ds(k0, Kg)], dev_v.at[me]),
            (obs.at[f], obs_v.at[me]),
        ][kind]

    for kind in range(4):
        def send_small(o, _):
            d = (me + o) % nb
            src, dst = small(kind, d)
            pltpu.make_async_remote_copy(
                src, dst, in_send.at[kind], in_recv.at[kind],
                device_id={"base": d}, device_id_type=MESH,
            ).start()
            return 0

        src, dst = small(kind, me)
        pltpu.make_async_copy(src, dst, in_recv.at[kind]).start()
        lax.fori_loop(1, nb, send_small, 0)

    def coh_block(d):
        return coh.at[d // g, pl.ds((d % g) * Kg, Kg)]

    pltpu.make_async_copy(coh_block(me), coh_v.at[me], coh_recv.at[me]).start()

    def send_coh(o, _):
        d = (me + o) % nb
        pltpu.make_async_remote_copy(
            coh_block(d), coh_v.at[me], coh_send, coh_recv.at[me],
            device_id={"base": d}, device_id_type=MESH,
        ).start()
        return 0

    lax.fori_loop(1, nb, send_coh, 0)

    wait_bytes(first_v, in_recv.at[0])
    wait_bytes(second_v, in_recv.at[1])

    def build(i, _):
        at = lax.broadcasted_iota(jnp.int32, (S, Bo), 0)
        onehot[i, :, 0:Bo] = jnp.where(at == first_v[i], 1.0, 0.0).astype(jnp.bfloat16)
        onehot[i, :, Bo : 2 * Bo] = jnp.where(at == second_v[i], 1.0, 0.0).astype(jnp.bfloat16)
        return 0

    lax.fori_loop(0, nb, build, 0)

    row = lax.broadcasted_iota(jnp.int32, (rows, rows), 0)
    col = lax.broadcasted_iota(jnp.int32, (rows, rows), 1)
    to_major = jnp.where(col == (row % Kg) * 8 + row // Kg, 1.0, 0.0)
    from_major = jnp.where(col == (row % 8) * Kg + row // 8, 1.0, 0.0)

    wait_bytes(dev_v, in_recv.at[2])
    for i in range(nb):
        acc[0:rows, i * So : (i + 1) * So] = dev_v[i].reshape(rows, So)
    start = jnp.dot(to_major, acc[0:rows], precision=HIGHEST, preferred_element_type=jnp.float32)
    which = lax.broadcasted_iota(jnp.int32, (rows, S), 0) // Kg
    jones[...] = start + jnp.where((which == 0) | (which == 6), 1.0, 0.0)
    wait_bytes(obs_v, in_recv.at[3])

    def owner(j):
        return {"band": j // F, "base": (j % F) * g + r}

    def t_copy(t, j):
        return pltpu.make_async_remote_copy(
            t_send.at[t, j], t_recv.at[t, mine], ts_sem.at[t, j], tr_sem.at[t, mine],
            device_id=owner(j), device_id_type=MESH,
        )

    def z_copy(t, f):
        return pltpu.make_async_remote_copy(
            z_send.at[t, f], z_recv.at[t, mine], zs_sem.at[t, f], zr_sem.at[t, mine],
            device_id=owner(f), device_id_type=MESH,
        )

    for t in range(ITERS):
        jj[...] = split_rows(jones[...])

        def send_models(q):
            for o in range(1, g):
                d = (r + o) % g
                pltpu.make_async_remote_copy(
                    model.at[t, pl.ds(q * cg, cg)], model_r.at[t, o - 1, pl.ds(q * cg, cg)],
                    m_send, m_recv.at[t, o - 1, q],
                    device_id={"base": s * g + d}, device_id_type=MESH,
                ).start()

        def forward(i, _):
            if t == 0:
                wait_bytes(coh_v.at[i], coh_recv.at[i])
                sky_rows = jnp.dot(
                    to_major, coh_v[i].reshape(rows, Bo), precision=HIGHEST,
                    preferred_element_type=jnp.float32,
                )
                cohc[i] = sky_rows
            else:
                sky_rows = cohc[i]
            both = jnp.dot(jj[...], onehot[i], preferred_element_type=jnp.float32)
            both = both[0:rows] + both[rows:]
            sky = components(sky_rows)
            leading = components(both[:, 0:Bo])
            trailing = components(both[:, Bo:])
            m = product(sky, trailing, adjoint_b=True)
            a = product(leading, sky)
            v = product(leading, m)
            left_t[i] = jnp.concatenate(flat(m), axis=0)
            right_t[i] = jnp.concatenate(flat(a), axis=0)
            model[t, i] = jnp.concatenate(
                [jnp.sum(x, axis=0, keepdims=True) for x in flat(v)], axis=0
            )
            return 0

        for q in range(groups):
            lax.fori_loop(q * cg, (q + 1) * cg, forward, 0)
            send_models(q)

        if t > 0:
            u = t - 1

            @pl.when(mine < npc)
            def _():
                for f in range(N):
                    wait_bytes(t_recv.at[u, f], tr_sem.at[u, f])
                coefficients = []
                for m in range(4):
                    total = float(basis[0, m]) * t_recv[u, 0]
                    for f in range(1, N):
                        total = total + float(basis[f, m]) * t_recv[u, f]
                    coefficients.append(total)
                for f in range(N):
                    value = float(basis[f, 0]) * coefficients[0]
                    for m in range(1, 4):
                        value = value + float(basis[f, m]) * coefficients[m]
                    z_send[u, f] = value
                for f in range(N):
                    @pl.when(mine != f)
                    def _():
                        z_copy(u, f).start()

                    @pl.when(mine == f)
                    def _():
                        pltpu.make_async_copy(z_send.at[u, f], z_recv.at[u, f], zr_sem.at[u, f]).start()

        acc[...] = jnp.zeros_like(acc)

        def backward(i, _):
            total = model[t, i]
            for o in range(1, g):
                total = total + model_r[t, o - 1, i]
            value = obs_v[i] - total
            if t == ITERS - 1:
                res[i] = value
            resid = components(value)
            gl = product(resid, components(left_t[i]), adjoint_b=True)
            gt = product(resid, components(right_t[i]), adjoint_a=True)
            both = jnp.concatenate(
                [jnp.concatenate(flat(gl), axis=0), jnp.concatenate(flat(gt), axis=0)], axis=1
            )
            acc[...] += lax.dot_general(
                split_rows(both), onehot[i], (((1,), (1,)), ((), ())),
                preferred_element_type=jnp.float32,
            )
            return 0

        for q in range(groups):
            for o in range(1, g):
                wait_bytes(model_r.at[t, o - 1, pl.ds(q * cg, cg)], m_recv.at[t, o - 1, q])
            lax.fori_loop(q * cg, (q + 1) * cg, backward, 0)

        if t == ITERS - 1:
            def send_res(f, _):
                d = f * g + r

                @pl.when(f != s)
                def _():
                    pltpu.make_async_remote_copy(
                        res.at[d], out_r.at[s], o_send.at[0], o_recv.at[0],
                        device_id={"base": d}, device_id_type=MESH,
                    ).start()

                @pl.when(f == s)
                def _():
                    pltpu.make_async_copy(res.at[d], out_r.at[s], o_recv.at[0]).start()

                return 0

            lax.fori_loop(0, F, send_res, 0)

        gradient = acc[0:rows] + acc[rows:]
        current = jones[...]
        if t == 0:
            updated = current + step * gradient
            target = updated
        else:
            u = t - 1
            for j in range(npc):
                wait_bytes(z_recv.at[u, j], zr_sem.at[u, j])
                r0, l0 = (j // lane_parts) * 8, (j % lane_parts) * L
                cons[r0 : r0 + 8, l0 : l0 + L] = z_recv[u, j]
            dual_var = penalty * (current - cons[...])
            if t > 1:
                dual_var = dual_var + dual[...]
            if t < ITERS - 1:
                dual[...] = dual_var
            updated = current + step * (gradient - dual_var - penalty * (current - cons[...]))
            target = updated + dual_var / penalty
        jones[...] = updated
        if t < ITERS - 1:
            for j in range(npc):
                r0, l0 = (j // lane_parts) * 8, (j % lane_parts) * L
                t_send[t, j] = target[r0 : r0 + 8, l0 : l0 + L]
            for j in range(npc):
                @pl.when(mine != j)
                def _():
                    t_copy(t, j).start()

                @pl.when(mine == j)
                def _():
                    pltpu.make_async_copy(t_send.at[t, j], t_recv.at[t, j], tr_sem.at[t, j]).start()

    final = jnp.dot(from_major, jones[...], precision=HIGHEST, preferred_element_type=jnp.float32)
    for d in range(nb):
        j_send[d] = final[:, d * So : (d + 1) * So].reshape(Kg, 8, So)
    place = out_j.at[s, pl.ds(r * Kg, Kg)]
    pltpu.make_async_copy(j_send.at[me], place, o_recv.at[1]).start()

    def send_jones(o, _):
        d = (me + o) % nb
        pltpu.make_async_remote_copy(
            j_send.at[d], place, o_send.at[1], o_recv.at[1],
            device_id={"base": d}, device_id_type=MESH,
        ).start()
        return 0

    lax.fori_loop(1, nb, send_jones, 0)

    for kind, buffer in enumerate([first_v, second_v, dev_v, obs_v]):
        wait_bytes(buffer.at[pl.ds(0, nb - 1)], in_send.at[kind])
    wait_bytes(coh_v.at[pl.ds(0, nb - 1)], coh_send)
    if g > 1:
        wait_bytes(model_r, m_send)
    for t in range(ITERS - 1):
        for j in range(npc):
            @pl.when(mine != j)
            def _():
                t_copy(t, j).wait_send()

        @pl.when(mine < npc)
        def _():
            for f in range(N):
                @pl.when(mine != f)
                def _():
                    z_copy(t, f).wait_send()
    wait_bytes(res.at[pl.ds(0, F - 1)], o_send.at[0])
    wait_bytes(j_send.at[pl.ds(0, nb - 1)], o_send.at[1])
    wait_bytes(out_r, o_recv.at[0])
    wait_bytes(j_send, o_recv.at[1])


def per_device(coherency, observed, jones_deviation, antenna_first, antenna_second):
    nb = lax.axis_size("base")
    nband = lax.axis_size("band")
    F, K, _, Bo = coherency.shape
    So = jones_deviation.shape[-1]
    S, B = So * nb, Bo * nb
    g = nb // F
    Kg = K // g
    rows = 8 * Kg
    N = F * nband
    step = STEP_GAIN * S / B
    penalty = PENALTY_GAIN * B / S
    lane_tiles = S // 128
    lane_parts = lane_tiles
    while lane_parts % 2 == 0 and Kg * lane_parts > N:
        lane_parts //= 2
    npc = Kg * lane_parts
    L = S // lane_parts
    groups = 4
    gp = max(g - 1, 1)
    cfg = (nb, nband, F, g, K, Kg, So, S, Bo, step, penalty, npc, lane_parts, groups)
    f32, bf16, i32 = jnp.float32, jnp.bfloat16, jnp.int32
    V, D = pltpu.VMEM, pltpu.SemaphoreType.DMA
    anywhere = pl.BlockSpec(memory_space=pl.ANY)
    return tuple(
        pl.pallas_call(
            functools.partial(kernel, cfg),
            out_shape=(
                jax.ShapeDtypeStruct((F, K, 8, So), f32),
                jax.ShapeDtypeStruct((F, 8, Bo), f32),
            ),
            in_specs=[anywhere] * 5,
            out_specs=(anywhere, anywhere),
            scratch_shapes=[
                V((nb, 1, Bo), i32),
                V((nb, 1, Bo), i32),
                V((nb, Kg, 8, So), f32),
                V((nb, 8, Bo), f32),
                V((nb, Kg, 8, Bo), f32),
                V((nb, S, 2 * Bo), bf16),
                V((nb, rows, Bo), f32),
                V((nb, rows, Bo), f32),
                V((nb, rows, Bo), f32),
                V((ITERS, nb, 8, Bo), f32),
                V((ITERS, gp, nb, 8, Bo), f32),
                V((2 * rows, S), bf16),
                V((rows, S), f32),
                V((rows, S), f32),
                V((rows, S), f32),
                V((2 * rows, S), f32),
                V((ITERS - 1, npc, 8, L), f32),
                V((ITERS - 1, N, 8, L), f32),
                V((ITERS - 1, N, 8, L), f32),
                V((ITERS - 1, npc, 8, L), f32),
                V((nb, 8, Bo), f32),
                V((nb, Kg, 8, So), f32),
                D((4,)),
                D((4,)),
                D,
                D((nb,)),
                D,
                D((ITERS, gp, groups)),
                D((ITERS - 1, npc)),
                D((ITERS - 1, N)),
                D((ITERS - 1, N)),
                D((ITERS - 1, npc)),
                D((2,)),
                D((2,)),
            ],
            compiler_params=pltpu.CompilerParams(
                collective_id=0, has_side_effects=True, vmem_limit_bytes=60 * 1024 * 1024
            ),
        )(
            coherency, observed, jones_deviation,
            antenna_first.reshape(1, Bo), antenna_second.reshape(1, Bo),
        )
    )


def solution(mesh):
    return jax.shard_map(
        per_device,
        mesh=mesh,
        in_specs=(
            P("band", None, None, "base"),
            P("band", None, "base"),
            P("band", None, None, "base"),
            P("base"),
            P("base"),
        ),
        out_specs=(P("band", None, None, "base"), P("band", None, "base")),
        check_vma=False,
    )
```

```python
import functools

import jax
import jax.numpy as jnp
import numpy as np
from jax import lax
from jax.experimental import pallas as pl
from jax.experimental.pallas import tpu as pltpu
from jax.sharding import PartitionSpec as P

ITERS = 3
STEP_GAIN = 1.2
PENALTY_GAIN = 0.25
MESH = pl.DeviceIdType.MESH
HIGHEST = lax.Precision.HIGHEST


def fit_basis(band_count):
    positions = ((2.0 * np.arange(band_count) + 1.0) / band_count - 1.0).astype(np.float64)
    columns = []
    for power in range(4):
        vector = positions**power
        for earlier in columns:
            vector = vector - np.sum(earlier * vector) * earlier
        columns.append(vector / np.sqrt(np.sum(vector * vector)))
    return np.stack(columns, axis=1)


def components(x):
    n = x.shape[0] // 8
    c = [x[i * n : (i + 1) * n] for i in range(8)]
    return [[(c[0], c[1]), (c[2], c[3])], [(c[4], c[5]), (c[6], c[7])]]


def flat(m):
    return [m[i][j][p] for i in range(2) for j in range(2) for p in range(2)]


def cmul(a, b):
    return (a[0] * b[0] - a[1] * b[1], a[0] * b[1] + a[1] * b[0])


def element_of(m, i, j, adjoint):
    return (m[j][i][0], -m[j][i][1]) if adjoint else m[i][j]


def product(a, b, adjoint_a=False, adjoint_b=False):
    rows = []
    for i in range(2):
        row = []
        for j in range(2):
            u = cmul(element_of(a, i, 0, adjoint_a), element_of(b, 0, j, adjoint_b))
            v = cmul(element_of(a, i, 1, adjoint_a), element_of(b, 1, j, adjoint_b))
            row.append((u[0] + v[0], u[1] + v[1]))
        rows.append(row)
    return rows


def split_rows(x):
    high = x.astype(jnp.bfloat16)
    low = (x - high.astype(jnp.float32)).astype(jnp.bfloat16)
    return jnp.concatenate([high, low], axis=0)


def wait_bytes(ref, sem):
    pltpu.make_async_copy(ref, ref, sem).wait()


def unpack_kernel(cfg, packed, residual_in, jones, residual):
    nb, g, Kg, So, fold = cfg
    k = Kg // fold
    for i in range(nb):
        for q in range(fold):
            at = (i % g) * Kg + q * k
            jones[i // g, at : at + k] = packed[i, :, q * So : (q + 1) * So].reshape(k, 8, So)
    residual[...] = residual_in[...]


def kernel(
    cfg,
    coh, obs, dev, first, second,
    out_p, out_r,
    dev_in, dev_s, first_v, second_v, dev_v, obs_v, coh_v,
    onehot, cohc, left_t, right_t, model, model_r,
    jj, jones, dual, cons, acc,
    t_send, t_recv, z_send, z_recv, res, j_send,
    dev_sem, in_send, in_recv, coh_send, coh_recv,
    m_send, m_recv, ts_sem, tr_sem, zs_sem, zr_sem, o_send, o_recv,
):
    nb, nband, F, g, K, Kg, So, S, Bo, step, penalty, npc, lane_parts, groups, fold = cfg
    rows = 8 * Kg
    short = rows // fold
    N = F * nband
    L = S // lane_parts
    basis = fit_basis(N)
    me = lax.axis_index("base")
    mb = lax.axis_index("band")
    s = me // g
    r = me % g
    mine = mb * F + s
    cg = nb // groups
    load_dev = pltpu.make_async_copy(dev, dev_in, dev_sem)
    load_dev.start()

    def chunk(p):
        return ((s - p // g + F) % F) * g + p % g

    def target_of(o):
        return ((s + o // g) % F) * g + (r + o) % g

    barrier = pltpu.get_barrier_semaphore()

    def greet(o, _):
        pl.semaphore_signal(barrier, inc=1, device_id={"base": (me + o) % nb}, device_id_type=MESH)
        return 0

    lax.fori_loop(1, nb, greet, 0)
    for ob in range(1, nband):
        def greet_band(f, _):
            pl.semaphore_signal(
                barrier, inc=1,
                device_id={"band": (mb + ob) % nband, "base": f * g + r}, device_id_type=MESH,
            )
            return 0

        lax.fori_loop(0, F, greet_band, 0)
    pl.semaphore_wait(barrier, nb - 1 + F * (nband - 1))

    def small(kind, d):
        f = d // g
        k0 = (d % g) * Kg
        return [
            (first, first_v.at[me]),
            (second, second_v.at[me]),
            (dev_s.at[d], dev_v.at[me]),
            (obs.at[f], obs_v.at[me]),
        ][kind]

    for kind in (0, 1, 3, 2):
        if kind == 2:
            load_dev.wait()

            def fold_block(d, _):
                block = dev_in[d // g, pl.ds((d % g) * Kg, Kg)].reshape(rows, So)
                for q in range(fold):
                    dev_s[d, :, q * So : (q + 1) * So] = block[q * short : (q + 1) * short]
                return 0

            lax.fori_loop(0, nb, fold_block, 0)

        def send_small(o, _):
            d = (me + o) % nb
            src, dst = small(kind, d)
            pltpu.make_async_remote_copy(
                src, dst, in_send.at[kind], in_recv.at[kind],
                device_id={"base": d}, device_id_type=MESH,
            ).start()
            return 0

        src, dst = small(kind, me)
        pltpu.make_async_copy(src, dst, in_recv.at[kind]).start()
        lax.fori_loop(1, nb, send_small, 0)

    def coh_block(d):
        return coh.at[d // g, pl.ds((d % g) * Kg, Kg)]

    pltpu.make_async_copy(coh_block(me), coh_v.at[me], coh_recv.at[me]).start()

    def send_coh(o, _):
        d = target_of(o)
        pltpu.make_async_remote_copy(
            coh_block(d), coh_v.at[me], coh_send, coh_recv.at[me],
            device_id={"base": d}, device_id_type=MESH,
        ).start()
        return 0

    lax.fori_loop(1, nb, send_coh, 0)

    wait_bytes(first_v, in_recv.at[0])
    wait_bytes(second_v, in_recv.at[1])

    def build(i, _):
        at = lax.broadcasted_iota(jnp.int32, (S, Bo), 0)
        onehot[i, :, 0:Bo] = jnp.where(at == first_v[i], 1.0, 0.0).astype(jnp.bfloat16)
        onehot[i, :, Bo : 2 * Bo] = jnp.where(at == second_v[i], 1.0, 0.0).astype(jnp.bfloat16)
        return 0

    lax.fori_loop(0, nb, build, 0)

    row = lax.broadcasted_iota(jnp.int32, (rows, rows), 0)
    col = lax.broadcasted_iota(jnp.int32, (rows, rows), 1)
    to_major = jnp.where(col == (row % Kg) * 8 + row // Kg, 1.0, 0.0)
    from_major = jnp.where(col == (row % 8) * Kg + row // 8, 1.0, 0.0)

    wait_bytes(dev_v, in_recv.at[2])
    for i in range(nb):
        for q in range(fold):
            acc[q * short : (q + 1) * short, i * So : (i + 1) * So] = dev_v[
                i, :, q * So : (q + 1) * So
            ]
    start = jnp.dot(to_major, acc[0:rows], precision=HIGHEST, preferred_element_type=jnp.float32)
    which = lax.broadcasted_iota(jnp.int32, (rows, S), 0) // Kg
    jones[...] = start + jnp.where((which == 0) | (which == 6), 1.0, 0.0)
    wait_bytes(obs_v, in_recv.at[3])

    def owner(j):
        return {"band": j // F, "base": (j % F) * g + r}

    def t_copy(t, j):
        return pltpu.make_async_remote_copy(
            t_send.at[t, j], t_recv.at[t, mine], ts_sem.at[t, j], tr_sem.at[t, mine],
            device_id=owner(j), device_id_type=MESH,
        )

    def z_copy(t, f):
        return pltpu.make_async_remote_copy(
            z_send.at[t, f], z_recv.at[t, mine], zs_sem.at[t, f], zr_sem.at[t, mine],
            device_id=owner(f), device_id_type=MESH,
        )

    for t in range(ITERS):
        jj[...] = split_rows(jones[...])

        def send_models(q):
            for o in range(1, g):
                d = (r + o) % g
                pltpu.make_async_remote_copy(
                    model.at[t, pl.ds(q * cg, cg)], model_r.at[t, o - 1, pl.ds(q * cg, cg)],
                    m_send, m_recv.at[t, o - 1, q],
                    device_id={"base": s * g + d}, device_id_type=MESH,
                ).start()

        def forward(p, _):
            i = chunk(p)
            if t == 0:
                wait_bytes(coh_v.at[i], coh_recv.at[i])
                sky_rows = jnp.dot(
                    to_major, coh_v[i].reshape(rows, Bo), precision=HIGHEST,
                    preferred_element_type=jnp.float32,
                )
                cohc[i] = sky_rows
            else:
                sky_rows = cohc[i]
            both = jnp.dot(jj[...], onehot[i], preferred_element_type=jnp.float32)
            both = both[0:rows] + both[rows:]
            sky = components(sky_rows)
            leading = components(both[:, 0:Bo])
            trailing = components(both[:, Bo:])
            m = product(sky, trailing, adjoint_b=True)
            a = product(leading, sky)
            v = product(leading, m)
            left_t[i] = jnp.concatenate(flat(m), axis=0)
            right_t[i] = jnp.concatenate(flat(a), axis=0)
            model[t, p] = jnp.concatenate(
                [jnp.sum(x, axis=0, keepdims=True) for x in flat(v)], axis=0
            )
            return 0

        acc[...] = jnp.zeros_like(acc)

        def backward(p, _):
            i = chunk(p)
            total = model[t, p]
            for o in range(1, g):
                total = total + model_r[t, o - 1, p]
            value = obs_v[i] - total
            if t == ITERS - 1:
                res[i] = value
            resid = components(value)
            gl = product(resid, components(left_t[i]), adjoint_b=True)
            gt = product(resid, components(right_t[i]), adjoint_a=True)
            both = jnp.concatenate(
                [jnp.concatenate(flat(gl), axis=0), jnp.concatenate(flat(gt), axis=0)], axis=1
            )
            acc[...] += lax.dot_general(
                split_rows(both), onehot[i], (((1,), (1,)), ((), ())),
                preferred_element_type=jnp.float32,
            )
            return 0

        def finish(q):
            for o in range(1, g):
                wait_bytes(model_r.at[t, o - 1, pl.ds(q * cg, cg)], m_recv.at[t, o - 1, q])
            lax.fori_loop(q * cg, (q + 1) * cg, backward, 0)

        for q in range(groups):
            lax.fori_loop(q * cg, (q + 1) * cg, forward, 0)
            send_models(q)
            if t == 0 and q > 0:
                finish(q - 1)

        if t > 0:
            u = t - 1

            @pl.when(mine < npc)
            def _():
                for f in range(N):
                    wait_bytes(t_recv.at[u, f], tr_sem.at[u, f])
                coefficients = []
                for m in range(4):
                    total = float(basis[0, m]) * t_recv[u, 0]
                    for f in range(1, N):
                        total = total + float(basis[f, m]) * t_recv[u, f]
                    coefficients.append(total)
                for f in range(N):
                    value = float(basis[f, 0]) * coefficients[0]
                    for m in range(1, 4):
                        value = value + float(basis[f, m]) * coefficients[m]
                    z_send[u, f] = value

                def send_z(o, _):
                    z_copy(u, (mine + o) % N).start()
                    return 0

                lax.fori_loop(1, N, send_z, 0)
                pltpu.make_async_copy(
                    z_send.at[u, mine], z_recv.at[u, mine], zr_sem.at[u, mine]
                ).start()

        for q in range(groups - 1 if t == 0 else 0, groups):
            finish(q)

        if t == ITERS - 1:
            def send_res(f, _):
                d = f * g + r

                @pl.when(f != s)
                def _():
                    pltpu.make_async_remote_copy(
                        res.at[d], out_r.at[s], o_send.at[0], o_recv.at[0],
                        device_id={"base": d}, device_id_type=MESH,
                    ).start()

                @pl.when(f == s)
                def _():
                    pltpu.make_async_copy(res.at[d], out_r.at[s], o_recv.at[0]).start()

                return 0

            lax.fori_loop(0, F, send_res, 0)

        gradient = acc[0:rows] + acc[rows:]
        current = jones[...]
        if t == 0:
            updated = current + step * gradient
            target = updated
        else:
            u = t - 1
            for j in range(npc):
                wait_bytes(z_recv.at[u, j], zr_sem.at[u, j])
                r0, l0 = (j // lane_parts) * 8, (j % lane_parts) * L
                cons[r0 : r0 + 8, l0 : l0 + L] = z_recv[u, j]
            dual_var = penalty * (current - cons[...])
            if t > 1:
                dual_var = dual_var + dual[...]
            if t < ITERS - 1:
                dual[...] = dual_var
            updated = current + step * (gradient - dual_var - penalty * (current - cons[...]))
            target = updated + dual_var / penalty
        jones[...] = updated
        if t < ITERS - 1:
            for j in range(npc):
                r0, l0 = (j // lane_parts) * 8, (j % lane_parts) * L
                t_send[t, j] = target[r0 : r0 + 8, l0 : l0 + L]

            def send_t(o, _):
                j = (mine + o) % N

                @pl.when(j < npc)
                def _():
                    t_copy(t, j).start()

                return 0

            lax.fori_loop(1, N, send_t, 0)

            @pl.when(mine < npc)
            def _():
                pltpu.make_async_copy(
                    t_send.at[t, mine], t_recv.at[t, mine], tr_sem.at[t, mine]
                ).start()

    final = jnp.dot(from_major, jones[...], precision=HIGHEST, preferred_element_type=jnp.float32)
    for d in range(nb):
        for q in range(fold):
            j_send[d, :, q * So : (q + 1) * So] = final[
                q * short : (q + 1) * short, d * So : (d + 1) * So
            ]
    place = out_p.at[me]
    pltpu.make_async_copy(j_send.at[me], place, o_recv.at[1]).start()

    def send_jones(o, _):
        d = (me + o) % nb
        pltpu.make_async_remote_copy(
            j_send.at[d], place, o_send.at[1], o_recv.at[1],
            device_id={"base": d}, device_id_type=MESH,
        ).start()
        return 0

    lax.fori_loop(1, nb, send_jones, 0)

    for kind, buffer in enumerate([first_v, second_v, dev_v, obs_v]):
        wait_bytes(buffer.at[pl.ds(0, nb - 1)], in_send.at[kind])
    wait_bytes(coh_v.at[pl.ds(0, nb - 1)], coh_send)
    if g > 1:
        wait_bytes(model_r, m_send)
    for t in range(ITERS - 1):
        for j in range(npc):
            @pl.when(mine != j)
            def _():
                t_copy(t, j).wait_send()

        @pl.when(mine < npc)
        def _():
            for f in range(N):
                @pl.when(mine != f)
                def _():
                    z_copy(t, f).wait_send()
    wait_bytes(res.at[pl.ds(0, F - 1)], o_send.at[0])
    wait_bytes(j_send.at[pl.ds(0, nb - 1)], o_send.at[1])
    wait_bytes(out_r, o_recv.at[0])
    wait_bytes(j_send, o_recv.at[1])


def per_device(coherency, observed, jones_deviation, antenna_first, antenna_second):
    nb = lax.axis_size("base")
    nband = lax.axis_size("band")
    F, K, _, Bo = coherency.shape
    So = jones_deviation.shape[-1]
    S, B = So * nb, Bo * nb
    g = nb // F
    Kg = K // g
    rows = 8 * Kg
    N = F * nband
    step = STEP_GAIN * S / B
    penalty = PENALTY_GAIN * B / S
    lane_tiles = S // 128
    lane_parts = lane_tiles
    while lane_parts % 2 == 0 and Kg * lane_parts > N:
        lane_parts //= 2
    npc = Kg * lane_parts
    L = S // lane_parts
    groups = 4
    fold = min(128 // So, Kg)
    gp = max(g - 1, 1)
    cfg = (nb, nband, F, g, K, Kg, So, S, Bo, step, penalty, npc, lane_parts, groups, fold)
    f32, bf16, i32 = jnp.float32, jnp.bfloat16, jnp.int32
    V, D = pltpu.VMEM, pltpu.SemaphoreType.DMA
    anywhere = pl.BlockSpec(memory_space=pl.ANY)
    packed, residual = (
        pl.pallas_call(
            functools.partial(kernel, cfg),
            out_shape=(
                jax.ShapeDtypeStruct((nb, rows // fold, fold * So), f32),
                jax.ShapeDtypeStruct((F, 8, Bo), f32),
            ),
            in_specs=[anywhere] * 5,
            out_specs=(anywhere, anywhere),
            scratch_shapes=[
                V((F, K, 8, So), f32),
                V((nb, rows // fold, fold * So), f32),
                V((nb, 1, Bo), i32),
                V((nb, 1, Bo), i32),
                V((nb, rows // fold, fold * So), f32),
                V((nb, 8, Bo), f32),
                V((nb, Kg, 8, Bo), f32),
                V((nb, S, 2 * Bo), bf16),
                V((nb, rows, Bo), f32),
                V((nb, rows, Bo), f32),
                V((nb, rows, Bo), f32),
                V((ITERS, nb, 8, Bo), f32),
                V((ITERS, gp, nb, 8, Bo), f32),
                V((2 * rows, S), bf16),
                V((rows, S), f32),
                V((rows, S), f32),
                V((rows, S), f32),
                V((2 * rows, S), f32),
                V((ITERS - 1, npc, 8, L), f32),
                V((ITERS - 1, N, 8, L), f32),
                V((ITERS - 1, N, 8, L), f32),
                V((ITERS - 1, npc, 8, L), f32),
                V((nb, 8, Bo), f32),
                V((nb, rows // fold, fold * So), f32),
                D,
                D((4,)),
                D((4,)),
                D,
                D((nb,)),
                D,
                D((ITERS, gp, groups)),
                D((ITERS - 1, npc)),
                D((ITERS - 1, N)),
                D((ITERS - 1, N)),
                D((ITERS - 1, npc)),
                D((2,)),
                D((2,)),
            ],
            compiler_params=pltpu.CompilerParams(
                collective_id=0, has_side_effects=True, vmem_limit_bytes=60 * 1024 * 1024
            ),
        )(
            coherency, observed, jones_deviation,
            antenna_first.reshape(1, Bo), antenna_second.reshape(1, Bo),
        )
    )
    return tuple(
        pl.pallas_call(
            functools.partial(unpack_kernel, (nb, g, Kg, So, fold)),
            out_shape=(
                jax.ShapeDtypeStruct((F, K, 8, So), f32),
                jax.ShapeDtypeStruct((F, 8, Bo), f32),
            ),
            in_specs=[pl.BlockSpec(memory_space=V)] * 2,
            out_specs=[pl.BlockSpec(memory_space=V)] * 2,
        )(packed, residual)
    )


def solution(mesh):
    return jax.shard_map(
        per_device,
        mesh=mesh,
        in_specs=(
            P("band", None, None, "base"),
            P("band", None, "base"),
            P("band", None, None, "base"),
            P("base"),
            P("base"),
        ),
        out_specs=(P("band", None, None, "base"), P("band", None, "base")),
        check_vma=False,
    )
```

```python
import functools

import jax
import jax.numpy as jnp
import numpy as np
from jax import lax
from jax.experimental import pallas as pl
from jax.experimental.pallas import tpu as pltpu
from jax.sharding import PartitionSpec as P

ITERS = 3
STEP_GAIN = 1.2
PENALTY_GAIN = 0.25
MESH = pl.DeviceIdType.MESH
HIGHEST = lax.Precision.HIGHEST


def fit_basis(band_count):
    positions = ((2.0 * np.arange(band_count) + 1.0) / band_count - 1.0).astype(np.float64)
    columns = []
    for power in range(4):
        vector = positions**power
        for earlier in columns:
            vector = vector - np.sum(earlier * vector) * earlier
        columns.append(vector / np.sqrt(np.sum(vector * vector)))
    return np.stack(columns, axis=1)


def components(x):
    n = x.shape[0] // 8
    c = [x[i * n : (i + 1) * n] for i in range(8)]
    return [[(c[0], c[1]), (c[2], c[3])], [(c[4], c[5]), (c[6], c[7])]]


def flat(m):
    return [m[i][j][p] for i in range(2) for j in range(2) for p in range(2)]


def cmul(a, b):
    return (a[0] * b[0] - a[1] * b[1], a[0] * b[1] + a[1] * b[0])


def element_of(m, i, j, adjoint):
    return (m[j][i][0], -m[j][i][1]) if adjoint else m[i][j]


def product(a, b, adjoint_a=False, adjoint_b=False):
    rows = []
    for i in range(2):
        row = []
        for j in range(2):
            u = cmul(element_of(a, i, 0, adjoint_a), element_of(b, 0, j, adjoint_b))
            v = cmul(element_of(a, i, 1, adjoint_a), element_of(b, 1, j, adjoint_b))
            row.append((u[0] + v[0], u[1] + v[1]))
        rows.append(row)
    return rows


def split_rows(x):
    high = x.astype(jnp.bfloat16)
    low = (x - high.astype(jnp.float32)).astype(jnp.bfloat16)
    return jnp.concatenate([high, low], axis=0)


def wait_bytes(ref, sem):
    pltpu.make_async_copy(ref, ref, sem).wait()


def unpack_kernel(cfg, packed, residual_in, jones, residual):
    nb, g, Kg, So, fold = cfg
    k = Kg // fold
    for i in range(nb):
        for q in range(fold):
            at = (i % g) * Kg + q * k
            jones[i // g, at : at + k] = packed[i, :, q * So : (q + 1) * So].reshape(k, 8, So)
    residual[...] = residual_in[...]


def kernel(
    cfg,
    coh, obs, dev, first, second,
    out_p, out_r,
    dev_in, dev_s, first_v, second_v, dev_v, obs_v, coh_v,
    onehot, cohc, left_t, right_t, model, model_r,
    jj, jones, dual, cons, acc,
    t_send, t_recv, z_send, z_recv, res, j_send,
    dev_sem, in_send, in_recv, coh_send, coh_recv,
    m_send, m_recv, ts_sem, tr_sem, zs_sem, zr_sem, o_send, o_recv,
):
    nb, nband, F, g, K, Kg, So, S, Bo, step, penalty, npc, lane_parts, groups, fold = cfg
    rows = 8 * Kg
    short = rows // fold
    N = F * nband
    L = S // lane_parts
    basis = fit_basis(N)
    me = lax.axis_index("base")
    mb = lax.axis_index("band")
    s = me // g
    r = me % g
    mine = mb * F + s
    cg = nb // groups
    unroll = 2
    load_dev = pltpu.make_async_copy(dev, dev_in, dev_sem)
    load_dev.start()

    def chunk(p):
        return ((s - p // g + F) % F) * g + p % g

    def target_of(o):
        return ((s + o // g) % F) * g + (r + o) % g

    barrier = pltpu.get_barrier_semaphore()

    def greet(o, _):
        pl.semaphore_signal(barrier, inc=1, device_id={"base": (me + o) % nb}, device_id_type=MESH)
        return 0

    lax.fori_loop(1, nb, greet, 0)
    for ob in range(1, nband):
        def greet_band(f, _):
            pl.semaphore_signal(
                barrier, inc=1,
                device_id={"band": (mb + ob) % nband, "base": f * g + r}, device_id_type=MESH,
            )
            return 0

        lax.fori_loop(0, F, greet_band, 0)
    pl.semaphore_wait(barrier, nb - 1 + F * (nband - 1))

    def small(kind, d):
        f = d // g
        k0 = (d % g) * Kg
        return [
            (first, first_v.at[me]),
            (second, second_v.at[me]),
            (dev_s.at[d], dev_v.at[me]),
            (obs.at[f], obs_v.at[me]),
        ][kind]

    for kind in (0, 1, 3, 2):
        if kind == 2:
            load_dev.wait()

            def fold_block(d, _):
                block = dev_in[d // g, pl.ds((d % g) * Kg, Kg)].reshape(rows, So)
                for q in range(fold):
                    dev_s[d, :, q * So : (q + 1) * So] = block[q * short : (q + 1) * short]
                return 0

            lax.fori_loop(0, nb, fold_block, 0)

        def send_small(o, _):
            d = (me + o) % nb
            src, dst = small(kind, d)
            pltpu.make_async_remote_copy(
                src, dst, in_send.at[kind], in_recv.at[kind],
                device_id={"base": d}, device_id_type=MESH,
            ).start()
            return 0

        src, dst = small(kind, me)
        pltpu.make_async_copy(src, dst, in_recv.at[kind]).start()
        lax.fori_loop(1, nb, send_small, 0)

    def coh_block(d):
        return coh.at[d // g, pl.ds((d % g) * Kg, Kg)]

    pltpu.make_async_copy(coh_block(me), coh_v.at[me], coh_recv.at[me]).start()

    def send_coh(o, _):
        d = target_of(o)
        pltpu.make_async_remote_copy(
            coh_block(d), coh_v.at[me], coh_send, coh_recv.at[me],
            device_id={"base": d}, device_id_type=MESH,
        ).start()
        return 0

    lax.fori_loop(1, nb, send_coh, 0)

    wait_bytes(first_v, in_recv.at[0])
    wait_bytes(second_v, in_recv.at[1])

    def build(i, _):
        at = lax.broadcasted_iota(jnp.int32, (S, Bo), 0)
        onehot[i, :, 0:Bo] = jnp.where(at == first_v[i], 1.0, 0.0).astype(jnp.bfloat16)
        onehot[i, :, Bo : 2 * Bo] = jnp.where(at == second_v[i], 1.0, 0.0).astype(jnp.bfloat16)
        return 0

    lax.fori_loop(0, nb, build, 0)

    row = lax.broadcasted_iota(jnp.int32, (rows, rows), 0)
    col = lax.broadcasted_iota(jnp.int32, (rows, rows), 1)
    to_major = jnp.where(col == (row % Kg) * 8 + row // Kg, 1.0, 0.0)
    from_major = jnp.where(col == (row % 8) * Kg + row // 8, 1.0, 0.0)

    wait_bytes(dev_v, in_recv.at[2])
    for i in range(nb):
        for q in range(fold):
            acc[q * short : (q + 1) * short, i * So : (i + 1) * So] = dev_v[
                i, :, q * So : (q + 1) * So
            ]
    start = jnp.dot(to_major, acc[0:rows], precision=HIGHEST, preferred_element_type=jnp.float32)
    which = lax.broadcasted_iota(jnp.int32, (rows, S), 0) // Kg
    jones[...] = start + jnp.where((which == 0) | (which == 6), 1.0, 0.0)
    wait_bytes(obs_v, in_recv.at[3])

    def owner(j):
        return {"band": j // F, "base": (j % F) * g + r}

    def t_copy(t, j):
        return pltpu.make_async_remote_copy(
            t_send.at[t, j], t_recv.at[t, mine], ts_sem.at[t, j], tr_sem.at[t, mine],
            device_id=owner(j), device_id_type=MESH,
        )

    def z_copy(t, f):
        return pltpu.make_async_remote_copy(
            z_send.at[t, f], z_recv.at[t, mine], zs_sem.at[t, f], zr_sem.at[t, mine],
            device_id=owner(f), device_id_type=MESH,
        )

    for t in range(ITERS):
        jj[...] = split_rows(jones[...])

        def send_models(q):
            for o in range(1, g):
                d = (r + o) % g
                pltpu.make_async_remote_copy(
                    model.at[t, pl.ds(q * cg, cg)], model_r.at[t, o - 1, pl.ds(q * cg, cg)],
                    m_send, m_recv.at[t, o - 1, q],
                    device_id={"base": s * g + d}, device_id_type=MESH,
                ).start()

        def forward(step_at, _):
            at = [step_at * unroll + n for n in range(unroll)]
            both, skies = [], []
            for p in at:
                i = chunk(p)
                if t == 0:
                    wait_bytes(coh_v.at[i], coh_recv.at[i])
                    cohc[p] = jnp.dot(
                        to_major, coh_v[i].reshape(rows, Bo), precision=HIGHEST,
                        preferred_element_type=jnp.float32,
                    )
                skies.append(cohc[p])
                both.append(jnp.dot(jj[...], onehot[i], preferred_element_type=jnp.float32))
            for p, pair, sky_rows in zip(at, both, skies):
                pair = pair[0:rows] + pair[rows:]
                sky = components(sky_rows)
                leading = components(pair[:, 0:Bo])
                trailing = components(pair[:, Bo:])
                m = product(sky, trailing, adjoint_b=True)
                a = product(leading, sky)
                v = product(leading, m)
                left_t[p] = jnp.concatenate(flat(m), axis=0)
                right_t[p] = jnp.concatenate(flat(a), axis=0)
                model[t, p] = jnp.concatenate(
                    [jnp.sum(x, axis=0, keepdims=True) for x in flat(v)], axis=0
                )
            return 0

        acc[...] = jnp.zeros_like(acc)

        def backward(step_at, _):
            update = None
            for n in range(unroll):
                p = step_at * unroll + n
                i = chunk(p)
                total = model[t, p]
                for o in range(1, g):
                    total = total + model_r[t, o - 1, p]
                value = obs_v[i] - total
                if t == ITERS - 1:
                    res[i] = value
                resid = components(value)
                gl = product(resid, components(left_t[p]), adjoint_b=True)
                gt = product(resid, components(right_t[p]), adjoint_a=True)
                both = jnp.concatenate(
                    [jnp.concatenate(flat(gl), axis=0), jnp.concatenate(flat(gt), axis=0)], axis=1
                )
                part = lax.dot_general(
                    split_rows(both), onehot[i], (((1,), (1,)), ((), ())),
                    preferred_element_type=jnp.float32,
                )
                update = part if update is None else update + part
            acc[...] += update
            return 0

        def finish(q):
            for o in range(1, g):
                wait_bytes(model_r.at[t, o - 1, pl.ds(q * cg, cg)], m_recv.at[t, o - 1, q])
            lax.fori_loop(q * cg // unroll, (q + 1) * cg // unroll, backward, 0)

        for q in range(groups):
            lax.fori_loop(q * cg // unroll, (q + 1) * cg // unroll, forward, 0)
            send_models(q)
            if t == 0 and q > 0:
                finish(q - 1)

        if t > 0:
            u = t - 1

            @pl.when(mine < npc)
            def _():
                for f in range(N):
                    wait_bytes(t_recv.at[u, f], tr_sem.at[u, f])
                coefficients = []
                for m in range(4):
                    total = float(basis[0, m]) * t_recv[u, 0]
                    for f in range(1, N):
                        total = total + float(basis[f, m]) * t_recv[u, f]
                    coefficients.append(total)
                for f in range(N):
                    value = float(basis[f, 0]) * coefficients[0]
                    for m in range(1, 4):
                        value = value + float(basis[f, m]) * coefficients[m]
                    z_send[u, f] = value

                def send_z(o, _):
                    z_copy(u, (mine + o) % N).start()
                    return 0

                lax.fori_loop(1, N, send_z, 0)
                pltpu.make_async_copy(
                    z_send.at[u, mine], z_recv.at[u, mine], zr_sem.at[u, mine]
                ).start()

        for q in range(groups - 1 if t == 0 else 0, groups):
            finish(q)

        if t == ITERS - 1:
            def send_res(f, _):
                d = f * g + r

                @pl.when(f != s)
                def _():
                    pltpu.make_async_remote_copy(
                        res.at[d], out_r.at[s], o_send.at[0], o_recv.at[0],
                        device_id={"base": d}, device_id_type=MESH,
                    ).start()

                @pl.when(f == s)
                def _():
                    pltpu.make_async_copy(res.at[d], out_r.at[s], o_recv.at[0]).start()

                return 0

            lax.fori_loop(0, F, send_res, 0)

        gradient = acc[0:rows] + acc[rows:]
        current = jones[...]
        if t == 0:
            updated = current + step * gradient
            target = updated
        else:
            u = t - 1
            for j in range(npc):
                wait_bytes(z_recv.at[u, j], zr_sem.at[u, j])
                r0, l0 = (j // lane_parts) * 8, (j % lane_parts) * L
                cons[r0 : r0 + 8, l0 : l0 + L] = z_recv[u, j]
            dual_var = penalty * (current - cons[...])
            if t > 1:
                dual_var = dual_var + dual[...]
            if t < ITERS - 1:
                dual[...] = dual_var
            updated = current + step * (gradient - dual_var - penalty * (current - cons[...]))
            target = updated + dual_var / penalty
        jones[...] = updated
        if t < ITERS - 1:
            for j in range(npc):
                r0, l0 = (j // lane_parts) * 8, (j % lane_parts) * L
                t_send[t, j] = target[r0 : r0 + 8, l0 : l0 + L]

            def send_t(o, _):
                j = (mine + o) % N

                @pl.when(j < npc)
                def _():
                    t_copy(t, j).start()

                return 0

            lax.fori_loop(1, N, send_t, 0)

            @pl.when(mine < npc)
            def _():
                pltpu.make_async_copy(
                    t_send.at[t, mine], t_recv.at[t, mine], tr_sem.at[t, mine]
                ).start()

    final = jnp.dot(from_major, jones[...], precision=HIGHEST, preferred_element_type=jnp.float32)
    for d in range(nb):
        for q in range(fold):
            j_send[d, :, q * So : (q + 1) * So] = final[
                q * short : (q + 1) * short, d * So : (d + 1) * So
            ]
    place = out_p.at[me]
    pltpu.make_async_copy(j_send.at[me], place, o_recv.at[1]).start()

    def send_jones(o, _):
        d = (me + o) % nb
        pltpu.make_async_remote_copy(
            j_send.at[d], place, o_send.at[1], o_recv.at[1],
            device_id={"base": d}, device_id_type=MESH,
        ).start()
        return 0

    lax.fori_loop(1, nb, send_jones, 0)

    for kind, buffer in enumerate([first_v, second_v, dev_v, obs_v]):
        wait_bytes(buffer.at[pl.ds(0, nb - 1)], in_send.at[kind])
    wait_bytes(coh_v.at[pl.ds(0, nb - 1)], coh_send)
    if g > 1:
        wait_bytes(model_r, m_send)
    for t in range(ITERS - 1):
        for j in range(npc):
            @pl.when(mine != j)
            def _():
                t_copy(t, j).wait_send()

        @pl.when(mine < npc)
        def _():
            for f in range(N):
                @pl.when(mine != f)
                def _():
                    z_copy(t, f).wait_send()
    wait_bytes(res.at[pl.ds(0, F - 1)], o_send.at[0])
    wait_bytes(j_send.at[pl.ds(0, nb - 1)], o_send.at[1])
    wait_bytes(out_r, o_recv.at[0])
    wait_bytes(j_send, o_recv.at[1])


def per_device(coherency, observed, jones_deviation, antenna_first, antenna_second):
    nb = lax.axis_size("base")
    nband = lax.axis_size("band")
    F, K, _, Bo = coherency.shape
    So = jones_deviation.shape[-1]
    S, B = So * nb, Bo * nb
    g = nb // F
    Kg = K // g
    rows = 8 * Kg
    N = F * nband
    step = STEP_GAIN * S / B
    penalty = PENALTY_GAIN * B / S
    lane_tiles = S // 128
    lane_parts = lane_tiles
    while lane_parts % 2 == 0 and Kg * lane_parts > N:
        lane_parts //= 2
    npc = Kg * lane_parts
    L = S // lane_parts
    groups = 4
    fold = min(128 // So, Kg)
    gp = max(g - 1, 1)
    cfg = (nb, nband, F, g, K, Kg, So, S, Bo, step, penalty, npc, lane_parts, groups, fold)
    f32, bf16, i32 = jnp.float32, jnp.bfloat16, jnp.int32
    V, D = pltpu.VMEM, pltpu.SemaphoreType.DMA
    anywhere = pl.BlockSpec(memory_space=pl.ANY)
    packed, residual = (
        pl.pallas_call(
            functools.partial(kernel, cfg),
            out_shape=(
                jax.ShapeDtypeStruct((nb, rows // fold, fold * So), f32),
                jax.ShapeDtypeStruct((F, 8, Bo), f32),
            ),
            in_specs=[anywhere] * 5,
            out_specs=(anywhere, anywhere),
            scratch_shapes=[
                V((F, K, 8, So), f32),
                V((nb, rows // fold, fold * So), f32),
                V((nb, 1, Bo), i32),
                V((nb, 1, Bo), i32),
                V((nb, rows // fold, fold * So), f32),
                V((nb, 8, Bo), f32),
                V((nb, Kg, 8, Bo), f32),
                V((nb, S, 2 * Bo), bf16),
                V((nb, rows, Bo), f32),
                V((nb, rows, Bo), f32),
                V((nb, rows, Bo), f32),
                V((ITERS, nb, 8, Bo), f32),
                V((ITERS, gp, nb, 8, Bo), f32),
                V((2 * rows, S), bf16),
                V((rows, S), f32),
                V((rows, S), f32),
                V((rows, S), f32),
                V((2 * rows, S), f32),
                V((ITERS - 1, npc, 8, L), f32),
                V((ITERS - 1, N, 8, L), f32),
                V((ITERS - 1, N, 8, L), f32),
                V((ITERS - 1, npc, 8, L), f32),
                V((nb, 8, Bo), f32),
                V((nb, rows // fold, fold * So), f32),
                D,
                D((4,)),
                D((4,)),
                D,
                D((nb,)),
                D,
                D((ITERS, gp, groups)),
                D((ITERS - 1, npc)),
                D((ITERS - 1, N)),
                D((ITERS - 1, N)),
                D((ITERS - 1, npc)),
                D((2,)),
                D((2,)),
            ],
            compiler_params=pltpu.CompilerParams(
                collective_id=0, has_side_effects=True, vmem_limit_bytes=60 * 1024 * 1024
            ),
        )(
            coherency, observed, jones_deviation,
            antenna_first.reshape(1, Bo), antenna_second.reshape(1, Bo),
        )
    )
    return tuple(
        pl.pallas_call(
            functools.partial(unpack_kernel, (nb, g, Kg, So, fold)),
            out_shape=(
                jax.ShapeDtypeStruct((F, K, 8, So), f32),
                jax.ShapeDtypeStruct((F, 8, Bo), f32),
            ),
            in_specs=[pl.BlockSpec(memory_space=V)] * 2,
            out_specs=[pl.BlockSpec(memory_space=V)] * 2,
        )(packed, residual)
    )


def solution(mesh):
    return jax.shard_map(
        per_device,
        mesh=mesh,
        in_specs=(
            P("band", None, None, "base"),
            P("band", None, "base"),
            P("band", None, None, "base"),
            P("base"),
            P("base"),
        ),
        out_specs=(P("band", None, None, "base"), P("band", None, "base")),
        check_vma=False,
    )
```
